32 devices in a mesh: space: 16 (over z, y, core), harm: 2 (over x).
Axes of the slice: x: 2, y: 2, z: 4, core: 2. Of those that a mesh axis runs over, the one named last changes fastest.
Arguments:
- coeffs: bfloat16 [120, 16, 256, 256], P('harm', 'space'), may hold values from -6 to 6
- synthesis: bfloat16 [256, 120], replicated, may hold values from -0.5 to 0.5
- projection: bfloat16 [120, 256], replicated, may hold values from -0.375 to 0.375
- turn_projection: bfloat16 [3, 120, 256], replicated, may hold values from -0.375 to 0.375
- damping: float32 [120], replicated, may hold values from 0.2 to 2
Outputs:
- rate: bfloat16 [120, 16, 256, 256], P('harm', 'space')
- velocity: float32 [3, 16, 256, 256], P(None, 'space', 'harm')
The draws below stay inside these ranges and needn't reach their ends.
All inputs are finite; a program needn't handle non-finite values.
Results may differ from the reference program's by a relative error of at most 0.0042.
Values may be sent and summed in bfloat16 or wider, within the bound.
A program may use at most 192 MiB of HBM per device.

```python
import math
import jax
import jax.numpy as jnp
from jax import lax

NX = 256
NY = 256
COEFS = 120
QUAD = 256
NZ = 16


def levels(own_key, extent, shards, smallest, high):
    factor_of, own = 1.0, jax.random.fold_in(own_key, 6)
    for dim, parts in shards:
        draws = jnp.exp(jax.random.uniform(jax.random.fold_in(own, dim), (parts,), jnp.float32, smallest / len(shards), high / len(shards)))
        factor_of = factor_of * jnp.repeat(draws, extent[dim] // parts).reshape([-1 if axis == dim else 1 for axis in range(len(extent))])
    return factor_of


def noise(stream_key, extent, deviation, limit, shards=(), held_as=jnp.bfloat16):
    loudness = levels(stream_key, extent, shards, -0.22, 0.18) if shards else 1.0
    values = jax.random.normal(stream_key, extent, jnp.float32) * deviation * loudness
    return jnp.minimum(jnp.maximum(values, -limit), limit).astype(held_as)


def setup_inputs(seed: int = 0) -> dict:
    streams_of = jax.random.split(jax.random.key(seed), 6)
    coeffs = noise(streams_of[0], (COEFS, NZ, NY, NX), 1.0, 6.0, ((0, 2), (1, 16)))
    synthesis = noise(streams_of[1], (QUAD, COEFS), COEFS ** -0.5, 0.5)
    projection = noise(streams_of[2], (COEFS, QUAD), QUAD ** -0.5, 0.375)
    turn_projection = noise(streams_of[3], (3, COEFS, QUAD), QUAD ** -0.5, 0.375)
    damping = jnp.clip(jnp.exp(jax.random.uniform(streams_of[4], (COEFS,), jnp.float32, math.log(0.2), math.log(2.0))), 0.2, 2.0)
    return {"coeffs": coeffs, "synthesis": synthesis, "projection": projection, "turn_projection": turn_projection, "damping": damping}


activity = -3.0
swim_speed = 1.0
transl_diff = 0.25
shape_factor = 0.9
golden_angle = math.pi * (3.0 - math.sqrt(5.0))
stress_pairs = ((0, 3, 4), (3, 1, 5), (4, 5, 2))

def sphere_directions(count):
    position = jnp.arange(count, dtype=jnp.float32)
    height = 1.0 - (2.0 * position + 1.0) / count
    radius = jnp.sqrt(1.0 - height * height)
    turning = position * golden_angle
    return jnp.stack([radius * jnp.cos(turning), radius * jnp.sin(turning), height])

def moment_table(synthesis, directions):
    dir_x, dir_y, dir_z = (directions[0], directions[1], directions[2])
    third = 1.0 / 3.0
    moments = jnp.stack([dir_x * dir_x - third, dir_y * dir_y - third, dir_z * dir_z - third, dir_x * dir_y, dir_x * dir_z, dir_y * dir_z])
    table = jnp.dot(moments, synthesis.astype(jnp.float32), precision=lax.Precision.HIGHEST)
    return (table * (activity / math.sqrt(synthesis.shape[0]))).astype(jnp.bfloat16)

def signed_wave(position, length):
    signed = jnp.where(position < length // 2, position, position - length)
    signed = jnp.where(position == length // 2, 0, signed)
    return 2.0 * math.pi / length * signed.astype(jnp.float32)

def differences(center, lower_z, upper_z, lower_y, upper_y):
    middle = center.astype(jnp.float32)
    upper_x = jnp.roll(middle, -1, 3)
    lower_x = jnp.roll(middle, 1, 3)
    lower_y = lower_y.astype(jnp.float32)
    upper_y = upper_y.astype(jnp.float32)
    lower_z = lower_z.astype(jnp.float32)
    upper_z = upper_z.astype(jnp.float32)
    gradients = ((0.5 * (upper_x - lower_x)).astype(jnp.bfloat16), (0.5 * (upper_y - lower_y)).astype(jnp.bfloat16), (0.5 * (upper_z - lower_z)).astype(jnp.bfloat16))
    laplacian = (upper_x + lower_x + upper_y + lower_y + upper_z + lower_z - 6.0 * middle).astype(jnp.bfloat16)
    return (gradients, laplacian)

def orient_rates(coef_block, gradients, laplacian, flow, directions, synthesis, projection, turn_projection, damping):
    density = jnp.dot(synthesis, coef_block, preferred_element_type=jnp.float32)
    advection = jnp.zeros_like(density)
    for j in range(3):
        slope = jnp.dot(synthesis, gradients[j], preferred_element_type=jnp.float32)
        advection = advection - (swim_speed * directions[j][:, None] + flow[j][None, :]) * slope
    strained = []
    for i in range(3):
        total = jnp.zeros_like(density)
        for j in range(3):
            forward_term = flow[3 + 3 * i + j]
            mirror_term = flow[3 + 3 * j + i]
            coupling = 0.5 * shape_factor * (forward_term + mirror_term) + 0.5 * (forward_term - mirror_term)
            total = total + coupling[None, :] * directions[j][:, None]
        strained.append(total)
    radial = directions[0][:, None] * strained[0] + directions[1][:, None] * strained[1] + directions[2][:, None] * strained[2]
    result = jnp.dot(projection, advection.astype(jnp.bfloat16), preferred_element_type=jnp.float32)
    for k in range(3):
        twist = ((strained[k] - directions[k][:, None] * radial) * density).astype(jnp.bfloat16)
        result = result + jnp.dot(turn_projection[k], twist, preferred_element_type=jnp.float32)
    result = result + transl_diff * laplacian.astype(jnp.float32) - damping[:, None] * coef_block.astype(jnp.float32)
    return result.astype(jnp.bfloat16)

def cell_rates(flat_coefs, flat_grads, flat_lap, flat_flow, directions, synthesis, projection, turn_projection, damping):
    cell_count = flat_coefs.shape[1]
    block_len = min(2048, cell_count)

    def advance(block_index, rate_cells):
        offset = block_index * block_len

        def window(array):
            return lax.dynamic_slice_in_dim(array, offset, block_len, 1)
        result = orient_rates(window(flat_coefs), tuple((window(g) for g in flat_grads)), window(flat_lap), window(flat_flow), directions, synthesis, projection, turn_projection, damping)
        return lax.dynamic_update_slice_in_dim(rate_cells, result, offset, 1)
    empty = jnp.zeros(flat_coefs.shape, jnp.bfloat16)
    return lax.fori_loop(0, cell_count // block_len, advance, empty)

def reference(coeffs, synthesis, projection, turn_projection, damping):
    directions = sphere_directions(QUAD)
    table = moment_table(synthesis, directions)
    stress = jnp.dot(table, coeffs.reshape(COEFS, -1), preferred_element_type=jnp.float32).reshape(6, NZ, NY, NX)
    spectrum = jnp.fft.fftn(stress, axes=(1, 2, 3))
    wave_x = signed_wave(jnp.arange(NX, dtype=jnp.int32), NX)[None, None, :]
    wave_y = signed_wave(jnp.arange(NY, dtype=jnp.int32), NY)[None, :, None]
    wave_z = signed_wave(jnp.arange(NZ, dtype=jnp.int32), NZ)[:, None, None]
    wave_vec = (wave_x, wave_y, wave_z)
    wave_sq = wave_x * wave_x + wave_y * wave_y + wave_z * wave_z
    inverse = jnp.where(wave_sq > 0, 1.0 / jnp.where(wave_sq > 0, wave_sq, 1.0), 0.0)
    force = []
    for i in range(3):
        total = spectrum[stress_pairs[i][0]] * wave_vec[0]
        total = total + spectrum[stress_pairs[i][1]] * wave_vec[1]
        total = total + spectrum[stress_pairs[i][2]] * wave_vec[2]
        force.append(1j * total)
    along = wave_vec[0] * force[0] + wave_vec[1] * force[1] + wave_vec[2] * force[2]
    flow_hat = [(force[i] - wave_vec[i] * along * inverse) * inverse for i in range(3)]
    pieces = list(flow_hat)
    for i in range(3):
        for j in range(3):
            pieces.append(1j * wave_vec[j] * flow_hat[i])
    fields = jnp.real(jnp.fft.ifftn(jnp.stack(pieces), axes=(1, 2, 3))).astype(jnp.float32)

    def one_plane(plane):
        center = lax.dynamic_index_in_dim(coeffs, plane, 1, True)
        lower_z = lax.dynamic_index_in_dim(coeffs, (plane + NZ - 1) % NZ, 1, True)
        upper_z = lax.dynamic_index_in_dim(coeffs, (plane + 1) % NZ, 1, True)
        gradients, laplacian = differences(center, lower_z, upper_z, jnp.roll(center, 1, 2), jnp.roll(center, -1, 2))
        flow = lax.dynamic_index_in_dim(fields, plane, 1, True).reshape(12, -1)
        return cell_rates(center.reshape(COEFS, -1), tuple((g.reshape(COEFS, -1) for g in gradients)), laplacian.reshape(COEFS, -1), flow, directions, synthesis, projection, turn_projection, damping)
    stacked = lax.map(one_plane, jnp.arange(NZ, dtype=jnp.int32))
    rate = jnp.transpose(stacked, (1, 0, 2)).reshape(COEFS, NZ, NY, NX)
    return (rate, fields[0:3])
```

```python
import math

import jax
import jax.numpy as jnp
from jax import lax
from jax.sharding import PartitionSpec as P

activity = -3.0
swim_speed = 1.0
transl_diff = 0.25
shape_factor = 0.9
golden_angle = math.pi * (3.0 - math.sqrt(5.0))
stress_pairs = ((0, 3, 4), (3, 1, 5), (4, 5, 2))


def with_halo(cells, sides, width):
    for axis, dim in sides:
        count = lax.axis_size(axis)
        head = lax.slice_in_dim(cells, 0, width, axis=dim)
        tail = lax.slice_in_dim(cells, cells.shape[dim] - width, cells.shape[dim], axis=dim)
        cells = jnp.concatenate(
            [
                lax.ppermute(tail, axis, [(i, (i + 1) % count) for i in range(count)]),
                cells,
                lax.ppermute(head, axis, [((i + 1) % count, i) for i in range(count)]),
            ],
            axis=dim,
        )
    return cells


def sphere_directions(count):
    position = jnp.arange(count, dtype=jnp.float32)
    height = 1.0 - (2.0 * position + 1.0) / count
    radius = jnp.sqrt(1.0 - height * height)
    turning = position * golden_angle
    return jnp.stack([radius * jnp.cos(turning), radius * jnp.sin(turning), height])


def moment_table(synthesis, directions):
    dir_x, dir_y, dir_z = (directions[0], directions[1], directions[2])
    third = 1.0 / 3.0
    moments = jnp.stack(
        [
            dir_x * dir_x - third,
            dir_y * dir_y - third,
            dir_z * dir_z - third,
            dir_x * dir_y,
            dir_x * dir_z,
            dir_y * dir_z,
        ]
    )
    table = jnp.dot(moments, synthesis.astype(jnp.float32), precision=lax.Precision.HIGHEST)
    return (table * (activity / math.sqrt(synthesis.shape[0]))).astype(jnp.bfloat16)


def signed_wave(position, length):
    signed = jnp.where(position < length // 2, position, position - length)
    signed = jnp.where(position == length // 2, 0, signed)
    return 2.0 * math.pi / length * signed.astype(jnp.float32)


def dft_tables(length, frequency):
    phase = jnp.arange(length, dtype=jnp.int32)[:, None] * frequency[None, :] % length
    angle = phase.astype(jnp.float32) * (2.0 * math.pi / length)
    return (jnp.cos(angle), jnp.sin(angle))


def differences(center, lower_z, upper_z, lower_y, upper_y):
    middle = center.astype(jnp.float32)
    upper_x = jnp.roll(middle, -1, 3)
    lower_x = jnp.roll(middle, 1, 3)
    lower_y = lower_y.astype(jnp.float32)
    upper_y = upper_y.astype(jnp.float32)
    lower_z = lower_z.astype(jnp.float32)
    upper_z = upper_z.astype(jnp.float32)
    gradients = (
        (0.5 * (upper_x - lower_x)).astype(jnp.bfloat16),
        (0.5 * (upper_y - lower_y)).astype(jnp.bfloat16),
        (0.5 * (upper_z - lower_z)).astype(jnp.bfloat16),
    )
    laplacian = (upper_x + lower_x + upper_y + lower_y + upper_z + lower_z - 6.0 * middle).astype(
        jnp.bfloat16
    )
    return (gradients, laplacian)


def composite_tables(directions, synthesis, projection, turn_projection):
    def through(weights):
        return jnp.dot(weights, synthesis.astype(jnp.float32), precision=lax.Precision.HIGHEST)

    project = projection.astype(jnp.float32)
    turning = turn_projection.astype(jnp.float32)
    radial = sum(turning[k] * directions[k] for k in range(3))
    tables = [through(-swim_speed * project * directions[j]) for j in range(3)]
    tables.append(through(-project))
    strain = [
        [through((turning[i] - radial * directions[i]) * directions[j]) for j in range(3)]
        for i in range(3)
    ]
    for i in range(3):
        for j in range(3):
            if i + j < 4:
                tables.append(strain[i][j] - strain[2][2] if i == j else strain[i][j])
    stacked = jnp.stack(tables, axis=1)
    coefs = stacked.shape[2]
    stacked = jnp.pad(stacked, ((0, 0), (0, 0), (0, -coefs % 16)))
    return stacked.astype(jnp.bfloat16).reshape(stacked.shape[0], -1)


def orient_rates(coef_block, gradients, laplacian, flow, tables, damping):
    middle = coef_block.astype(jnp.float32)
    carried = sum(flow[j][None, :] * gradients[j].astype(jnp.float32) for j in range(3))
    inputs = [*gradients, carried.astype(jnp.bfloat16)]
    for i in range(3):
        for j in range(3):
            if i + j < 4:
                forward_term = flow[3 + 3 * i + j]
                mirror_term = flow[3 + 3 * j + i]
                coupling = 0.5 * shape_factor * (forward_term + mirror_term) + 0.5 * (
                    forward_term - mirror_term
                )
                inputs.append((coupling[None, :] * middle).astype(jnp.bfloat16))
    extra = -coef_block.shape[0] % 16
    inputs = jnp.concatenate([jnp.pad(x, ((0, extra), (0, 0))) for x in inputs], axis=0)
    result = jnp.dot(tables, inputs, preferred_element_type=jnp.float32)
    result = result + transl_diff * laplacian.astype(jnp.float32) - damping[:, None] * middle
    return result.astype(jnp.bfloat16)


def cell_rates(flat_coefs, flat_grads, flat_lap, flat_flow, tables, damping):
    cell_count = flat_coefs.shape[1]
    block_len = min(2048, cell_count)

    def advance(block_index, rate_cells):
        offset = block_index * block_len

        def window(array):
            return lax.dynamic_slice_in_dim(array, offset, block_len, 1)

        result = orient_rates(
            window(flat_coefs),
            tuple((window(g) for g in flat_grads)),
            window(flat_lap),
            window(flat_flow),
            tables,
            damping,
        )
        return lax.dynamic_update_slice_in_dim(rate_cells, result, offset, 1)

    empty = jnp.zeros(flat_coefs.shape, jnp.bfloat16)
    return lax.fori_loop(0, cell_count // block_len, advance, empty)


def stokes_fields(stress, spaces, groups, space_id, group_id):
    highest = lax.Precision.HIGH
    length_x = stress.shape[3]
    packed = (length_x // 2) % (spaces * groups) == 0
    slots = length_x // 2 if packed else length_x
    cos_x, sin_x = dft_tables(length_x, jnp.arange(slots, dtype=jnp.int32))
    parity = 1.0 - 2.0 * (jnp.arange(length_x, dtype=jnp.int32) % 2).astype(jnp.float32)
    sin_x = -sin_x
    if packed:
        sin_x = sin_x.at[:, 0].set(parity)
    real_part = jnp.einsum("abcn,nm->ambc", stress, cos_x, precision=highest)
    imag_part = jnp.einsum("abcn,nm->ambc", stress, sin_x, precision=highest)
    columns = lax.all_to_all(
        lax.all_to_all(
            jnp.stack([real_part, imag_part]).astype(jnp.bfloat16), "space", split_axis=2, concat_axis=3, tiled=True
        ),
        "harm",
        split_axis=2,
        concat_axis=4,
        tiled=True,
    )
    columns = columns.astype(jnp.float32)
    real_part, imag_part = (columns[0], columns[1])
    columns_dev = columns.shape[2]
    length_z = columns.shape[3]
    length_y = columns.shape[4]
    cos_y, sin_y = dft_tables(length_y, jnp.arange(length_y, dtype=jnp.int32))
    cos_z, sin_z = dft_tables(length_z, jnp.arange(length_z, dtype=jnp.int32))
    real_next = jnp.einsum("ajzn,nm->ajzm", real_part, cos_y, precision=highest) + jnp.einsum(
        "ajzn,nm->ajzm", imag_part, sin_y, precision=highest
    )
    imag_next = jnp.einsum("ajzn,nm->ajzm", imag_part, cos_y, precision=highest) - jnp.einsum(
        "ajzn,nm->ajzm", real_part, sin_y, precision=highest
    )
    real_part = jnp.einsum("ajny,nm->ajmy", real_next, cos_z, precision=highest) + jnp.einsum(
        "ajny,nm->ajmy", imag_next, sin_z, precision=highest
    )
    imag_part = jnp.einsum("ajny,nm->ajmy", imag_next, cos_z, precision=highest) - jnp.einsum(
        "ajny,nm->ajmy", real_next, sin_z, precision=highest
    )
    column_freq = (
        space_id * groups * columns_dev
        + group_id * columns_dev
        + jnp.arange(columns_dev, dtype=jnp.int32)
    )
    wave_x = signed_wave(column_freq, length_x)[:, None, None]
    wave_y = signed_wave(jnp.arange(length_y, dtype=jnp.int32), length_y)[None, None, :]
    wave_z = signed_wave(jnp.arange(length_z, dtype=jnp.int32), length_z)[None, :, None]
    wave_vec = (wave_x, wave_y, wave_z)
    wave_sq = wave_x * wave_x + wave_y * wave_y + wave_z * wave_z
    inverse = jnp.where(wave_sq > 0, 1.0 / jnp.where(wave_sq > 0, wave_sq, 1.0), 0.0)
    force_real = []
    force_imag = []
    for i in range(3):
        sum_real = (
            real_part[stress_pairs[i][0]] * wave_vec[0]
            + real_part[stress_pairs[i][1]] * wave_vec[1]
            + real_part[stress_pairs[i][2]] * wave_vec[2]
        )
        sum_imag = (
            imag_part[stress_pairs[i][0]] * wave_vec[0]
            + imag_part[stress_pairs[i][1]] * wave_vec[1]
            + imag_part[stress_pairs[i][2]] * wave_vec[2]
        )
        force_real.append(-sum_imag)
        force_imag.append(sum_real)
    along_real = (
        wave_vec[0] * force_real[0] + wave_vec[1] * force_real[1] + wave_vec[2] * force_real[2]
    )
    along_imag = (
        wave_vec[0] * force_imag[0] + wave_vec[1] * force_imag[1] + wave_vec[2] * force_imag[2]
    )
    flow_real = [(force_real[i] - wave_vec[i] * along_real * inverse) * inverse for i in range(3)]
    flow_imag = [(force_imag[i] - wave_vec[i] * along_imag * inverse) * inverse for i in range(3)]
    pieces_real = list(flow_real)
    pieces_imag = list(flow_imag)
    for i in range(3):
        for j in range(1, 3 if i < 2 else 2):
            pieces_real.append(-wave_vec[j] * flow_imag[i])
            pieces_imag.append(wave_vec[j] * flow_real[i])
    real_part = jnp.stack(pieces_real)
    imag_part = jnp.stack(pieces_imag)
    real_next = jnp.einsum("ajny,nm->ajmy", real_part, cos_z, precision=highest) - jnp.einsum(
        "ajny,nm->ajmy", imag_part, sin_z, precision=highest
    )
    imag_next = jnp.einsum("ajny,nm->ajmy", imag_part, cos_z, precision=highest) + jnp.einsum(
        "ajny,nm->ajmy", real_part, sin_z, precision=highest
    )
    real_part = jnp.einsum("ajzn,nm->ajzm", real_next, cos_y, precision=highest) - jnp.einsum(
        "ajzn,nm->ajzm", imag_next, sin_y, precision=highest
    )
    imag_part = jnp.einsum("ajzn,nm->ajzm", imag_next, cos_y, precision=highest) + jnp.einsum(
        "ajzn,nm->ajzm", real_next, sin_y, precision=highest
    )
    returned = lax.all_to_all(
        lax.all_to_all(
            jnp.stack([real_part, imag_part]).astype(jnp.bfloat16), "space", split_axis=3, concat_axis=2, tiled=True
        ),
        "harm",
        split_axis=4,
        concat_axis=2,
        tiled=True,
    )
    returned = returned.astype(jnp.float32)
    position = jnp.arange(slots, dtype=jnp.int32)
    owner_group = position // (spaces * columns_dev)
    owner_space = position // columns_dev % spaces
    owner_column = position % columns_dev
    return_freq = owner_space * groups * columns_dev + owner_group * columns_dev + owner_column
    cos_back, sin_back = dft_tables(length_x, return_freq)
    from_real, from_imag = cos_back, -sin_back
    if packed:
        first = (return_freq == 0)[None, :]
        from_real = jnp.where(first, 1.0, 2.0 * from_real)
        from_imag = jnp.where(first, parity[:, None], 2.0 * from_imag)
    scale = 1.0 / (length_x * length_y * length_z)
    from_real, from_imag = from_real * scale, from_imag * scale
    wave_back = signed_wave(return_freq, length_x)[None, :]

    def back(pieces_real, pieces_imag, table_real, table_imag):
        return jnp.einsum("akbc,nk->abcn", pieces_real, table_real, precision=highest) + jnp.einsum(
            "akbc,nk->abcn", pieces_imag, table_imag, precision=highest
        )

    plain = back(returned[0], returned[1], from_real, from_imag)
    along_x = back(returned[0, :3], returned[1, :3], wave_back * from_imag, -wave_back * from_real)
    velocity, others = plain[:3], plain[3:]
    trace_rest = -(along_x[0] + others[2])
    return jnp.stack(
        [
            velocity[0],
            velocity[1],
            velocity[2],
            along_x[0],
            others[0],
            others[1],
            along_x[1],
            others[2],
            others[3],
            along_x[2],
            others[4],
            trace_rest,
        ]
    )


def local(coeffs, synthesis, projection, turn_projection, damping):
    spaces = lax.axis_size("space")
    groups = lax.axis_size("harm")
    space_id = lax.axis_index("space")
    group_id = lax.axis_index("harm")
    local_coefs, planes, length_y, length_x = coeffs.shape
    total_coefs = synthesis.shape[1]
    directions = sphere_directions(synthesis.shape[0])
    table = moment_table(synthesis, directions)
    regrouped = lax.all_to_all(coeffs, "harm", split_axis=2, concat_axis=0, tiled=True)
    padded = with_halo(regrouped, (("space", 1), ("harm", 2)), 1)
    gradients, laplacian = differences(
        regrouped,
        padded[:, :-2, 1:-1],
        padded[:, 2:, 1:-1],
        padded[:, 1:-1, :-2],
        padded[:, 1:-1, 2:],
    )
    cell_shape = regrouped.shape
    own_table = lax.dynamic_slice_in_dim(table, group_id * local_coefs, local_coefs, 1)
    partial_stress = jnp.dot(
        own_table, coeffs.reshape(local_coefs, -1), preferred_element_type=jnp.float32
    )
    partial_stress = partial_stress.reshape(6, planes, length_y, length_x)
    stress = lax.psum_scatter(partial_stress, "harm", scatter_dimension=2, tiled=True)
    fields = stokes_fields(stress, spaces, groups, space_id, group_id)
    rate_cells = cell_rates(
        regrouped.reshape(total_coefs, -1),
        tuple((g.reshape(total_coefs, -1) for g in gradients)),
        laplacian.reshape(total_coefs, -1),
        fields.reshape(12, -1),
        composite_tables(directions, synthesis, projection, turn_projection),
        damping,
    )
    rate = lax.all_to_all(
        rate_cells.reshape(cell_shape), "harm", split_axis=0, concat_axis=2, tiled=True
    )
    return (rate, fields[0:3])


def solution(mesh):
    in_specs = (P("harm", "space", None, None), P(), P(), P(), P())
    out_specs = (P("harm", "space", None, None), P(None, "space", "harm", None))
    return jax.shard_map(local, mesh=mesh, in_specs=in_specs, out_specs=out_specs, check_vma=False)
```
